32 devices in a mesh: parts: 2 (over y), coef: 4 (over z), poly: 2 (over x), limb: 2 (over core).
Axes of the slice: x: 2, y: 2, z: 4, core: 2. Of those that a mesh axis runs over, the one named last changes fastest.
Arguments:
- coefficients: float32 [96, 128, 4096], P(('parts', 'poly', 'limb'), None, 'coef'), parts along dimension 0, may hold values from -6 to 6
- batch_weights: float32 [32, 48], P('parts', ('poly', 'limb')), parts along dimension 0, may hold values from -0.875 to 0.875
- claimed: float32 [2, 32, 48], P(None, 'parts', ('poly', 'limb')), parts along dimension 1, may hold values from -6 to 6
- point_index: int32 [32], P(('parts', 'poly', 'limb')), parts along dimension 0, may hold values from 0 to 524287
- point_cycle: int32 [32], P(('parts', 'poly', 'limb')), parts along dimension 0, may hold values from 0 to 3
Outputs:
- evaluations: float32 [2, 128, 96, 32, 128], P(None, 'coef', ('parts', 'poly', 'limb')), parts along dimension 2
- quotient: float32 [2, 32, 128, 4096], P(None, ('parts', 'poly', 'limb'), None, 'coef'), parts along dimension 1
The draws below stay inside these ranges and needn't reach their ends.
There are 2 independent parts, one for each index of `parts`. The reference program is written for one: setup_inputs(seed, part) draws one part's arguments, and reference() takes and returns one part's arrays. A program takes and returns all parts, laid end to end along the dimension named above; each array names one. Nothing has to cross between parts.
All inputs are finite; a program needn't handle non-finite values.
Results may differ from the reference program's by a relative error of at most 0.0003.
Values sent between devices are 32-bit elements; how exact they have to be, the bound alone decides.
A program may use at most 128 MiB of HBM per device.

```python
import math
import jax
import jax.numpy as jnp
from jax import lax

POLYS = 48
COLUMNS = 16
LEN_COLS = 128
SPLIT_HI = 32
SPLIT_LO = 128
LEN_ROWS = 4096
LENGTH = 524288


def with_ends(result, key, least, top_value):
    shape = result.shape
    place = [jax.random.randint(jax.random.fold_in(key, axis), (), 0, shape[axis]) for axis in range(len(shape))]
    result = result.at[tuple(place)].set(least)
    longest = shape.index(max(shape))
    place[longest] = (place[longest] + 1) % shape[longest]
    return result.at[tuple(place)].set(top_value)


def steps_of(rng, extent, split, smallest, largest):
    def one(axis_at, blocks):
        steps = jax.random.uniform(jax.random.fold_in(jax.random.fold_in(rng, 6), axis_at), (blocks,), jnp.float32, smallest / len(split), largest / len(split))
        return jnp.repeat(jnp.exp(steps), extent[axis_at] // blocks).reshape((-1,) + (1,) * (len(extent) - axis_at - 1))

    factor_of = one(*split[0])
    for cut in split[1:]:
        factor_of = factor_of * one(*cut)
    return factor_of


def centred(own_key, dims, scale, reach, pieces=(), held_as=jnp.bfloat16):
    entries = jax.random.normal(own_key, dims, jnp.float32) * scale
    if len(pieces) > 0:
        entries = steps_of(own_key, dims, pieces, -0.22, 0.18) * entries
    return jnp.clip(entries, min=-reach, max=reach).astype(held_as)


def setup_inputs(seed: int = 0, part: int = 0) -> dict:
    keys = jax.random.split(jax.random.key(seed), 6)
    part_keys = jax.random.split(jax.random.fold_in(keys[5], part), 6)
    return {
        "coefficients": centred(part_keys[0], (POLYS, LEN_COLS, LEN_ROWS), 1.0, 6.0, ((0, 4), (2, 4)), jnp.float32),
        "batch_weights": centred(part_keys[1], (COLUMNS, POLYS), POLYS ** -0.5, 0.875, ((1, 4),), jnp.float32),
        "claimed": centred(part_keys[2], (2, COLUMNS, POLYS), 1.0, 6.0, ((2, 4),), jnp.float32),
        "point_index": with_ends(jax.random.randint(part_keys[3], (COLUMNS,), 0, LENGTH), jax.random.fold_in(part_keys[3], 1), 0, LENGTH - 1).astype(jnp.int32),
        "point_cycle": with_ends(jax.random.randint(part_keys[4], (COLUMNS,), 0, 4), jax.random.fold_in(part_keys[4], 1), 0, 3).astype(jnp.int32),
    }


def arrange(values):
    return values.reshape(POLYS, SPLIT_LO, SPLIT_HI, LEN_COLS).transpose(3, 0, 2, 1)

def reference(coefficients, batch_weights, claimed, point_index, point_cycle):
    root_length = math.sqrt(LENGTH)
    flattened = coefficients.reshape(POLYS, LENGTH)
    spectrum = jnp.fft.fft(flattened, axis=1) / root_length
    spec_real = jnp.real(spectrum)
    spec_imag = jnp.imag(spectrum)
    evaluations = jnp.stack([arrange(spec_real), arrange(spec_imag)])
    offsets = lax.optimization_barrier(jnp.sum(batch_weights[None] * claimed, axis=2))
    numer_real = jnp.dot(batch_weights, spec_real, precision=lax.Precision.HIGHEST) - offsets[0][:, None]
    numer_imag = jnp.dot(batch_weights, spec_imag, precision=lax.Precision.HIGHEST) - offsets[1][:, None]
    positions = jnp.arange(LENGTH, dtype=jnp.int32)
    angles = positions.astype(jnp.float32) * (2.0 * math.pi / LENGTH)
    point_angle = point_index.astype(jnp.float32) * (2.0 * math.pi / LENGTH)
    radius = 1.0 + (point_cycle.astype(jnp.float32) + 1.0) / 512.0
    diff_real = jnp.cos(angles)[None, :] - (radius * jnp.cos(point_angle))[:, None]
    diff_imag = (radius * jnp.sin(point_angle))[:, None] - jnp.sin(angles)[None, :]
    magnitude = diff_real * diff_real + diff_imag * diff_imag
    quot_real = (numer_real * diff_real + numer_imag * diff_imag) / magnitude
    quot_imag = (numer_imag * diff_real - numer_real * diff_imag) / magnitude
    coeffs = jnp.fft.ifft(quot_real + 1j * quot_imag, axis=1) * root_length
    quotient = jnp.stack([jnp.real(coeffs), jnp.imag(coeffs)]).reshape(2, COLUMNS, LEN_COLS, LEN_ROWS)
    return (evaluations, quotient)
```

```python
import functools
import math

import jax
import jax.numpy as jnp
from jax import lax
from jax.experimental import pallas as pl
from jax.experimental.pallas import tpu as pltpu
from jax.sharding import PartitionSpec as P

SPLIT_HI = 32
SPLIT_LO = 128
CHUNKS = 4

precise = lax.Precision.HIGHEST


def phase_table(row_index, col_index, length):
    product = row_index[:, None] * col_index[None, :] % length
    angles = product.astype(jnp.float32) * (2.0 * math.pi / length)
    return (jnp.cos(angles), jnp.sin(angles))


def cost(flops, moved):
    return pl.CostEstimate(flops=flops, bytes_accessed=moved, transcendentals=0)


def first_kernel(mat_ref, cos_ref, sin_ref, x_ref, out_ref):
    targets, _, _, groups, per_target, lanes = out_ref.shape
    extent = targets * per_target
    for g in range(groups):
        cols = slice(g * lanes, (g + 1) * lanes)
        both = jnp.dot(mat_ref[...], x_ref[0, :, cols], precision=precise,
                       preferred_element_type=jnp.float32)
        real, imag = both[:extent], both[extent:]
        cos_turn, sin_turn = cos_ref[:, cols], sin_ref[:, cols]
        turned_real = real * cos_turn + imag * sin_turn
        turned_imag = imag * cos_turn - real * sin_turn
        for t in range(targets):
            rows = slice(t * per_target, (t + 1) * per_target)
            out_ref[t, 0, 0, g] = turned_real[rows]
            out_ref[t, 0, 1, g] = turned_imag[rows]


def first_section(values, tables, start, count, targets):
    matrix, cos_turn, sin_turn = tables
    _, extent, rows_here = values.shape
    groups = rows_here // SPLIT_LO
    per_target = extent // targets
    shape = (targets, count, 2, groups, per_target, SPLIT_LO)
    block = (targets, 1, 2, groups, per_target, SPLIT_LO)
    size = count * 2 * extent * rows_here
    return pl.pallas_call(
        first_kernel,
        grid=(count,),
        in_specs=[
            pl.BlockSpec((2 * extent, extent), lambda p: (0, 0)),
            pl.BlockSpec((extent, rows_here), lambda p: (0, 0)),
            pl.BlockSpec((extent, rows_here), lambda p: (0, 0)),
            pl.BlockSpec((1, extent, rows_here), lambda p: (start + p, 0, 0)),
        ],
        out_specs=pl.BlockSpec(block, lambda p: (0, p, 0, 0, 0, 0)),
        out_shape=jax.ShapeDtypeStruct(shape, jnp.float32),
        compiler_params=pltpu.CompilerParams(vmem_limit_bytes=24 << 20),
        cost_estimate=cost(size * extent * 12, size * 6),
        name="first_section",
    )(matrix, cos_turn, sin_turn, values)


def fft(pieces):
    count = len(pieces)
    if count == 1:
        return pieces
    even, odd = fft(pieces[0::2]), fft(pieces[1::2])
    low, high = [], []
    for k in range(count // 2):
        er, ei = even[k]
        orr, oi = odd[k]
        if k == 0:
            tr, ti = orr, oi
        elif 4 * k == count:
            tr, ti = oi, -orr
        else:
            c = math.cos(2 * math.pi * k / count)
            s = math.sin(2 * math.pi * k / count)
            if 8 * k == count:
                tr, ti = (orr + oi) * c, (oi - orr) * c
            elif 8 * k == 3 * count:
                tr, ti = (oi - orr) * s, (orr + oi) * (-s)
            else:
                tr, ti = orr * c + oi * s, oi * c - orr * s
        low.append((er + tr, ei + ti))
        high.append((er - tr, ei - ti))
    return low + high


def second_kernel(mat_ref, cos_ref, sin_ref, in_ref, *rest):
    out_ref, real_ref, imag_ref = rest[-3:]
    sources, _, _, groups, here, lanes = in_ref.shape
    pieces = [
        (in_ref[s, 0, 0, g], in_ref[s, 0, 1, g]) for s in range(sources) for g in range(groups)
    ]
    for v, (real, imag) in enumerate(fft(pieces)):
        cos_turn, sin_turn = cos_ref[v : v + 1], sin_ref[v : v + 1]
        at = pl.ds(v, here, stride=SPLIT_HI)
        real_ref[at, :] = real * cos_turn + imag * sin_turn
        imag_ref[at, :] = imag * cos_turn - real * sin_turn
    both = jnp.concatenate([real_ref[...], imag_ref[...]], axis=1)
    done = jnp.dot(both, mat_ref[...], precision=precise, preferred_element_type=jnp.float32)
    out_ref[0, :, 0] = done[:, :lanes].reshape(here, SPLIT_HI, lanes)
    out_ref[1, :, 0] = done[:, lanes:].reshape(here, SPLIT_HI, lanes)


def second_section(received, tables, start, total, held):
    matrix, cos_turn, sin_turn = tables
    sources, count, _, groups, per_target, lanes = received.shape
    here = min(8, per_target)
    out_shape = jax.ShapeDtypeStruct((2, per_target, total, SPLIT_HI, lanes), jnp.float32)
    size = received.size
    operands = [matrix, cos_turn, sin_turn, received]
    in_specs = [
        pl.BlockSpec(matrix.shape, lambda p, k: (0, 0)),
        pl.BlockSpec(cos_turn.shape, lambda p, k: (0, 0)),
        pl.BlockSpec(sin_turn.shape, lambda p, k: (0, 0)),
        pl.BlockSpec((sources, 1, 2, groups, here, lanes), lambda p, k: (0, p, 0, 0, k, 0)),
    ]
    aliases = {}
    if held is not None:
        operands.append(held)
        in_specs.append(pl.BlockSpec(memory_space=pl.ANY))
        aliases = {4: 0}
    return pl.pallas_call(
        second_kernel,
        grid=(count, per_target // here),
        in_specs=in_specs,
        out_specs=pl.BlockSpec(
            (2, here, 1, SPLIT_HI, lanes), lambda p, k: (0, k, start + p, 0, 0)
        ),
        out_shape=out_shape,
        scratch_shapes=[pltpu.VMEM((SPLIT_HI * here, lanes), jnp.float32)] * 2,
        input_output_aliases=aliases,
        compiler_params=pltpu.CompilerParams(vmem_limit_bytes=16 << 20),
        cost_estimate=cost(size * 2 * lanes * 12, size * 8),
        name="second_section",
    )(*operands)


def combine_kernel(weight_ref, x_ref, out_ref):
    columns, polys = weight_ref.shape
    for g in range(x_ref.shape[2] // SPLIT_LO):
        cols = slice(g * SPLIT_LO, (g + 1) * SPLIT_LO)
        rows = [x_ref[p, :, cols] for p in range(polys)]
        for j in range(columns):
            total = rows[0] * weight_ref[j, 0]
            for p in range(1, polys):
                total = total + rows[p] * weight_ref[j, p]
            out_ref[j, :, cols] = total


def combine(weights, values):
    polys, extent, rows_here = values.shape
    columns = weights.shape[0]
    size = extent * rows_here
    return pl.pallas_call(
        combine_kernel,
        grid=(extent // 8,),
        in_specs=[
            pl.BlockSpec(memory_space=pltpu.SMEM),
            pl.BlockSpec((polys, 8, rows_here), lambda n: (0, n, 0)),
        ],
        out_specs=pl.BlockSpec((columns, 8, rows_here), lambda n: (0, n, 0)),
        out_shape=jax.ShapeDtypeStruct((columns, extent, rows_here), jnp.float32),
        compiler_params=pltpu.CompilerParams(vmem_limit_bytes=16 << 20),
        cost_estimate=cost(size * columns * polys * 20, size * 4 * (columns + polys)),
        name="combine",
    )(weights, values)


def powers(exponents, point_index, log_radius, length):
    shape = (-1,) + (1,) * exponents.ndim
    phase = (exponents[None] * point_index.reshape(shape)) & (length - 1)
    angles = phase.astype(jnp.float32) * (2.0 * math.pi / length)
    size = jnp.exp(-exponents[None].astype(jnp.float32) * log_radius.reshape(shape))
    return size * jnp.cos(angles), size * jnp.sin(angles)


def quotient_kernel(matrix_ref, step_ref, carry_ref, c_ref, out_ref):
    rows, width = c_ref.shape[1:]
    lanes = step_ref.shape[2]
    step_real, step_imag = step_ref[0, 0:1], step_ref[0, 1:2]
    carry = carry_ref[0]
    carry_real, carry_imag = carry[:, 0:1], carry[:, 1:2]
    for g in range(width // lanes):
        cols = slice(g * lanes, (g + 1) * lanes)
        local = jnp.dot(c_ref[0, :, cols], matrix_ref[0], precision=precise,
                        preferred_element_type=jnp.float32)
        real = local[:, :lanes] + (step_real * carry_real - step_imag * carry_imag)
        imag = local[:, lanes:] + (step_real * carry_imag + step_imag * carry_real)
        out_ref[0, 0, :, cols] = real
        out_ref[1, 0, :, cols] = imag
        carry_real, carry_imag = real[:, lanes - 1 :], imag[:, lanes - 1 :]


def quotient_section(combined, offsets, point_index, point_cycle, owners):
    columns, extent, rows_here = combined.shape
    length = extent * rows_here * owners
    lanes = SPLIT_LO
    log_radius = jnp.log1p((point_cycle.astype(jnp.float32) + 1.0) / 512.0)
    power = functools.partial(
        powers, point_index=point_index, log_radius=log_radius, length=length
    )
    index = jnp.arange(lanes, dtype=jnp.int32)
    ahead = index[None, :] - index[:, None] + 1
    below = (ahead > 0)[None]
    local_real, local_imag = power(jnp.maximum(ahead, 0))
    matrix = jnp.concatenate(
        [jnp.where(below, -local_real, 0.0), jnp.where(below, -local_imag, 0.0)], axis=2
    )
    step = jnp.stack(power(index + 1), axis=1)
    end_real, end_imag = power(rows_here - jnp.arange(rows_here, dtype=jnp.int32))
    ends = jnp.stack(
        [
            -jnp.sum(combined * end_real[:, None, :], axis=2),
            -jnp.sum(combined * end_imag[:, None, :], axis=2),
        ]
    )
    gathered = lax.all_gather(ends, "coef")
    me = lax.axis_index("coef")
    shift = offsets * math.sqrt(length)
    turn_real, turn_imag = power(jnp.full((), rows_here, jnp.int32))
    first = jnp.stack(
        [
            turn_real * shift[0] - turn_imag * shift[1],
            turn_real * shift[1] + turn_imag * shift[0],
        ]
    )
    gathered = gathered.at[0, :, :, 0].add(first)
    row = jnp.arange(extent, dtype=jnp.int32)
    owner = jnp.arange(owners, dtype=jnp.int32)
    segments = extent * owners
    away = (
        (row[:, None, None] * owners + me)
        - (row[None, None, :] * owners + owner[None, :, None])
        - 1
        + segments
    ) % segments
    pass_real, pass_imag = power(away * rows_here)
    whole = 1.0 - power(jnp.full((), length, jnp.int32))[0]
    ends_real = jnp.transpose(gathered[:, 0], (1, 0, 2))[:, None]
    ends_imag = jnp.transpose(gathered[:, 1], (1, 0, 2))[:, None]
    carry_real = jnp.sum(pass_real * ends_real - pass_imag * ends_imag, axis=(2, 3))
    carry_imag = jnp.sum(pass_real * ends_imag + pass_imag * ends_real, axis=(2, 3))
    carry = jnp.stack([carry_real, carry_imag], axis=2) / whole[:, None, None]
    starts = ((row == 0) & (me == 0))[None, :, None]
    carry = carry + jnp.where(starts, shift.T[:, None, :], 0.0)
    size = columns * extent * rows_here
    return pl.pallas_call(
        quotient_kernel,
        grid=(columns,),
        in_specs=[
            pl.BlockSpec((1, lanes, 2 * lanes), lambda j: (j, 0, 0)),
            pl.BlockSpec((1, 2, lanes), lambda j: (j, 0, 0)),
            pl.BlockSpec((1, extent, 2), lambda j: (j, 0, 0)),
            pl.BlockSpec((1, extent, rows_here), lambda j: (j, 0, 0)),
        ],
        out_specs=pl.BlockSpec((2, 1, extent, rows_here), lambda j: (0, j, 0, 0)),
        out_shape=jax.ShapeDtypeStruct((2, columns, extent, rows_here), jnp.float32),
        compiler_params=pltpu.CompilerParams(vmem_limit_bytes=16 << 20),
        cost_estimate=cost(size * 4 * lanes * 6, size * 12),
        name="quotient",
    )(matrix, step, carry, combined)


def transform_tables(extent, rows_here, length):
    index = jnp.arange(extent, dtype=jnp.int32)
    cos_table, sin_table = phase_table(index, index, extent)
    first_matrix = jnp.concatenate([cos_table, -sin_table]) * (1.0 / math.sqrt(extent))
    row_index = lax.axis_index("coef") * rows_here + jnp.arange(rows_here, dtype=jnp.int32)
    cos_turn, sin_turn = phase_table(index, row_index, length)
    slow = jnp.arange(SPLIT_HI, dtype=jnp.int32)
    fast = jnp.arange(SPLIT_LO, dtype=jnp.int32)
    cos_row, sin_row = phase_table(slow, fast, SPLIT_HI * SPLIT_LO)
    cos_fast, sin_fast = phase_table(fast, fast, SPLIT_LO)
    second_matrix = jnp.concatenate(
        [
            jnp.concatenate([cos_fast, -sin_fast], axis=1),
            jnp.concatenate([sin_fast, cos_fast], axis=1),
        ]
    ) * (1.0 / math.sqrt(SPLIT_HI * SPLIT_LO))
    return (first_matrix, cos_turn, sin_turn), (second_matrix, cos_row, sin_row)


def shards(owners, coefficients, batch_weights, claimed, point_index, point_cycle):
    polys, extent, rows_here = coefficients.shape
    length = extent * rows_here * owners
    first_tables, second_tables = transform_tables(extent, rows_here, length)
    chunks = math.gcd(CHUNKS, polys)
    count = polys // chunks
    received = []
    for i in range(chunks):
        sent = first_section(coefficients, first_tables, i * count, count, owners)
        received.append(lax.all_to_all(sent, "coef", split_axis=0, concat_axis=0, tiled=True))

    combined = combine(batch_weights, coefficients)
    combined_here = lax.psum_scatter(
        combined, ("poly", "limb"), scatter_dimension=0, tiled=True
    )
    offsets = jnp.sum(batch_weights[None] * claimed, axis=2)
    offsets_here = lax.psum_scatter(
        offsets, ("poly", "limb"), scatter_dimension=1, tiled=True
    )
    quotient = quotient_section(combined_here, offsets_here, point_index, point_cycle, owners)

    evaluations = None
    for i in range(chunks):
        evaluations = second_section(
            received[i], second_tables, i * count, polys, evaluations
        )
    return (evaluations, quotient)


def solution(mesh):
    placed = (
        P(("parts", "poly", "limb"), None, "coef"),
        P("parts", ("poly", "limb")),
        P(None, "parts", ("poly", "limb")),
        P(("parts", "poly", "limb")),
        P(("parts", "poly", "limb")),
    )
    return jax.shard_map(
        functools.partial(shards, mesh.shape["coef"]),
        mesh=mesh,
        in_specs=placed,
        out_specs=(
            P(None, "coef", ("parts", "poly", "limb"), None, None),
            P(None, ("parts", "poly", "limb"), None, "coef"),
        ),
        check_vma=False,
    )
```

```python
import functools
import math

import jax
import jax.numpy as jnp
from jax import lax
from jax.experimental import pallas as pl
from jax.experimental.pallas import tpu as pltpu
from jax.sharding import PartitionSpec as P

SPLIT_HI = 32
SPLIT_LO = 128
SHARE = 6

precise = lax.Precision.HIGHEST


def phase_table(row_index, col_index, length):
    product = row_index[:, None] * col_index[None, :] % length
    angles = product.astype(jnp.float32) * (2.0 * math.pi / length)
    return (jnp.cos(angles), jnp.sin(angles))


def cost(flops, moved):
    return pl.CostEstimate(flops=flops, bytes_accessed=moved, transcendentals=0)


def first_kernel(mat_ref, cos_ref, sin_ref, x_ref, out_ref):
    targets, _, _, groups, per_target, lanes = out_ref.shape
    extent = targets * per_target
    for g in range(groups):
        cols = slice(g * lanes, (g + 1) * lanes)
        both = jnp.dot(mat_ref[...], x_ref[0, :, cols], precision=precise,
                       preferred_element_type=jnp.float32)
        real, imag = both[:extent], both[extent:]
        cos_turn, sin_turn = cos_ref[:, cols], sin_ref[:, cols]
        turned_real = real * cos_turn + imag * sin_turn
        turned_imag = imag * cos_turn - real * sin_turn
        for t in range(targets):
            rows = slice(t * per_target, (t + 1) * per_target)
            out_ref[t, 0, 0, g] = turned_real[rows]
            out_ref[t, 0, 1, g] = turned_imag[rows]


def first_section(values, tables, start, count, targets):
    matrix, cos_turn, sin_turn = tables
    _, extent, rows_here = values.shape
    groups = rows_here // SPLIT_LO
    per_target = extent // targets
    shape = (targets, count, 2, groups, per_target, SPLIT_LO)
    block = (targets, 1, 2, groups, per_target, SPLIT_LO)
    size = count * 2 * extent * rows_here
    return pl.pallas_call(
        first_kernel,
        grid=(count,),
        in_specs=[
            pl.BlockSpec((2 * extent, extent), lambda p: (0, 0)),
            pl.BlockSpec((extent, rows_here), lambda p: (0, 0)),
            pl.BlockSpec((extent, rows_here), lambda p: (0, 0)),
            pl.BlockSpec((1, extent, rows_here), lambda p: (start + p, 0, 0)),
        ],
        out_specs=pl.BlockSpec(block, lambda p: (0, p, 0, 0, 0, 0)),
        out_shape=jax.ShapeDtypeStruct(shape, jnp.float32),
        compiler_params=pltpu.CompilerParams(vmem_limit_bytes=60 << 20),
        cost_estimate=cost(size * extent * 12, size * 6),
        name="first_section",
    )(matrix, cos_turn, sin_turn, values)


def fft(pieces):
    count = len(pieces)
    if count == 1:
        return pieces
    even, odd = fft(pieces[0::2]), fft(pieces[1::2])
    low, high = [], []
    for k in range(count // 2):
        er, ei = even[k]
        orr, oi = odd[k]
        if k == 0:
            tr, ti = orr, oi
        elif 4 * k == count:
            tr, ti = oi, -orr
        else:
            c = math.cos(2 * math.pi * k / count)
            s = math.sin(2 * math.pi * k / count)
            if 8 * k == count:
                tr, ti = (orr + oi) * c, (oi - orr) * c
            elif 8 * k == 3 * count:
                tr, ti = (oi - orr) * s, (orr + oi) * (-s)
            else:
                tr, ti = orr * c + oi * s, oi * c - orr * s
        low.append((er + tr, ei + ti))
        high.append((er - tr, ei - ti))
    return low + high


def second_kernel(mat_ref, cos_ref, sin_ref, in_ref, *rest):
    out_ref, real_ref, imag_ref = rest[-3:]
    sources, _, _, groups, here, lanes = in_ref.shape
    pieces = [
        (in_ref[s, 0, 0, g], in_ref[s, 0, 1, g]) for s in range(sources) for g in range(groups)
    ]
    for v, (real, imag) in enumerate(fft(pieces)):
        cos_turn, sin_turn = cos_ref[v : v + 1], sin_ref[v : v + 1]
        at = pl.ds(v, here, stride=SPLIT_HI)
        real_ref[at, :] = real * cos_turn + imag * sin_turn
        imag_ref[at, :] = imag * cos_turn - real * sin_turn
    both = jnp.concatenate([real_ref[...], imag_ref[...]], axis=1)
    done = jnp.dot(both, mat_ref[...], precision=precise, preferred_element_type=jnp.float32)
    out_ref[0, :, 0] = done[:, :lanes].reshape(here, SPLIT_HI, lanes)
    out_ref[1, :, 0] = done[:, lanes:].reshape(here, SPLIT_HI, lanes)


def second_section(received, tables, start, total, held):
    matrix, cos_turn, sin_turn = tables
    sources, count, _, groups, per_target, lanes = received.shape
    here = min(8, per_target)
    out_shape = jax.ShapeDtypeStruct((2, per_target, total, SPLIT_HI, lanes), jnp.float32)
    size = received.size
    operands = [matrix, cos_turn, sin_turn, received]
    in_specs = [
        pl.BlockSpec(matrix.shape, lambda p, k: (0, 0)),
        pl.BlockSpec(cos_turn.shape, lambda p, k: (0, 0)),
        pl.BlockSpec(sin_turn.shape, lambda p, k: (0, 0)),
        pl.BlockSpec((sources, 1, 2, groups, here, lanes), lambda p, k: (0, p, 0, 0, k, 0)),
    ]
    aliases = {}
    if held is not None:
        operands.append(held)
        in_specs.append(pl.BlockSpec(memory_space=pl.ANY))
        aliases = {4: 0}
    return pl.pallas_call(
        second_kernel,
        grid=(count, per_target // here),
        in_specs=in_specs,
        out_specs=pl.BlockSpec(
            (2, here, 1, SPLIT_HI, lanes), lambda p, k: (0, k, start + p, 0, 0)
        ),
        out_shape=out_shape,
        scratch_shapes=[pltpu.VMEM((SPLIT_HI * here, lanes), jnp.float32)] * 2,
        input_output_aliases=aliases,
        compiler_params=pltpu.CompilerParams(vmem_limit_bytes=16 << 20),
        cost_estimate=cost(size * 2 * lanes * 12, size * 8),
        name="second_section",
    )(*operands)


def combine_kernel(weight_ref, x_ref, out_ref):
    columns, polys = weight_ref.shape
    for g in range(x_ref.shape[2] // SPLIT_LO):
        cols = slice(g * SPLIT_LO, (g + 1) * SPLIT_LO)
        rows = [x_ref[p, :, cols] for p in range(polys)]
        for j in range(columns):
            total = rows[0] * weight_ref[j, 0]
            for p in range(1, polys):
                total = total + rows[p] * weight_ref[j, p]
            out_ref[j, :, cols] = total


def combine(weights, values):
    polys, extent, rows_here = values.shape
    columns = weights.shape[0]
    size = extent * rows_here
    return pl.pallas_call(
        combine_kernel,
        grid=(extent // 8,),
        in_specs=[
            pl.BlockSpec(memory_space=pltpu.SMEM),
            pl.BlockSpec((polys, 8, rows_here), lambda n: (0, n, 0)),
        ],
        out_specs=pl.BlockSpec((columns, 8, rows_here), lambda n: (0, n, 0)),
        out_shape=jax.ShapeDtypeStruct((columns, extent, rows_here), jnp.float32),
        compiler_params=pltpu.CompilerParams(vmem_limit_bytes=60 << 20),
        cost_estimate=cost(size * columns * polys * 20, size * 4 * (columns + polys)),
        name="combine",
    )(weights, values)


def powers(exponents, point_index, log_radius, length):
    shape = (-1,) + (1,) * exponents.ndim
    phase = (exponents[None] * point_index.reshape(shape)) & (length - 1)
    angles = phase.astype(jnp.float32) * (2.0 * math.pi / length)
    size = jnp.exp(-exponents[None].astype(jnp.float32) * log_radius.reshape(shape))
    return size * jnp.cos(angles), size * jnp.sin(angles)


def quotient_kernel(matrix_ref, step_ref, carry_ref, c_ref, out_ref):
    rows, width = c_ref.shape[1:]
    lanes = step_ref.shape[2]
    step_real, step_imag = step_ref[0, 0:1], step_ref[0, 1:2]
    carry = carry_ref[0]
    carry_real, carry_imag = carry[:, 0:1], carry[:, 1:2]
    for g in range(width // lanes):
        cols = slice(g * lanes, (g + 1) * lanes)
        local = jnp.dot(c_ref[0, :, cols], matrix_ref[0], precision=precise,
                        preferred_element_type=jnp.float32)
        real = local[:, :lanes] + (step_real * carry_real - step_imag * carry_imag)
        imag = local[:, lanes:] + (step_real * carry_imag + step_imag * carry_real)
        out_ref[0, 0, :, cols] = real
        out_ref[1, 0, :, cols] = imag
        carry_real, carry_imag = real[:, lanes - 1 :], imag[:, lanes - 1 :]


def quotient_section(combined, offsets, point_index, point_cycle, owners):
    columns, extent, rows_here = combined.shape
    length = extent * rows_here * owners
    lanes = SPLIT_LO
    log_radius = jnp.log1p((point_cycle.astype(jnp.float32) + 1.0) / 512.0)
    power = functools.partial(
        powers, point_index=point_index, log_radius=log_radius, length=length
    )
    index = jnp.arange(lanes, dtype=jnp.int32)
    ahead = index[None, :] - index[:, None] + 1
    below = (ahead > 0)[None]
    local_real, local_imag = power(jnp.maximum(ahead, 0))
    matrix = jnp.concatenate(
        [jnp.where(below, -local_real, 0.0), jnp.where(below, -local_imag, 0.0)], axis=2
    )
    step = jnp.stack(power(index + 1), axis=1)
    end_real, end_imag = power(rows_here - jnp.arange(rows_here, dtype=jnp.int32))
    ends = jnp.stack(
        [
            -jnp.sum(combined * end_real[:, None, :], axis=2),
            -jnp.sum(combined * end_imag[:, None, :], axis=2),
        ]
    )
    gathered = lax.all_gather(ends, "coef")
    me = lax.axis_index("coef")
    shift = offsets * math.sqrt(length)
    turn_real, turn_imag = power(jnp.full((), rows_here, jnp.int32))
    first = jnp.stack(
        [
            turn_real * shift[0] - turn_imag * shift[1],
            turn_real * shift[1] + turn_imag * shift[0],
        ]
    )
    gathered = gathered.at[0, :, :, 0].add(first)
    row = jnp.arange(extent, dtype=jnp.int32)
    owner = jnp.arange(owners, dtype=jnp.int32)
    segments = extent * owners
    away = (
        (row[:, None, None] * owners + me)
        - (row[None, None, :] * owners + owner[None, :, None])
        - 1
        + segments
    ) % segments
    pass_real, pass_imag = power(away * rows_here)
    whole = 1.0 - power(jnp.full((), length, jnp.int32))[0]
    ends_real = jnp.transpose(gathered[:, 0], (1, 0, 2))[:, None]
    ends_imag = jnp.transpose(gathered[:, 1], (1, 0, 2))[:, None]
    carry_real = jnp.sum(pass_real * ends_real - pass_imag * ends_imag, axis=(2, 3))
    carry_imag = jnp.sum(pass_real * ends_imag + pass_imag * ends_real, axis=(2, 3))
    carry = jnp.stack([carry_real, carry_imag], axis=2) / whole[:, None, None]
    starts = ((row == 0) & (me == 0))[None, :, None]
    carry = carry + jnp.where(starts, shift.T[:, None, :], 0.0)
    size = columns * extent * rows_here
    return pl.pallas_call(
        quotient_kernel,
        grid=(columns,),
        in_specs=[
            pl.BlockSpec((1, lanes, 2 * lanes), lambda j: (j, 0, 0)),
            pl.BlockSpec((1, 2, lanes), lambda j: (j, 0, 0)),
            pl.BlockSpec((1, extent, 2), lambda j: (j, 0, 0)),
            pl.BlockSpec((1, extent, rows_here), lambda j: (j, 0, 0)),
        ],
        out_specs=pl.BlockSpec((2, 1, extent, rows_here), lambda j: (0, j, 0, 0)),
        out_shape=jax.ShapeDtypeStruct((2, columns, extent, rows_here), jnp.float32),
        compiler_params=pltpu.CompilerParams(vmem_limit_bytes=16 << 20),
        cost_estimate=cost(size * 4 * lanes * 6, size * 12),
        name="quotient",
    )(matrix, step, carry, combined)


def transform_tables(extent, rows_here, length):
    index = jnp.arange(extent, dtype=jnp.int32)
    cos_table, sin_table = phase_table(index, index, extent)
    first_matrix = jnp.concatenate([cos_table, -sin_table]) * (1.0 / math.sqrt(extent))
    row_index = lax.axis_index("coef") * rows_here + jnp.arange(rows_here, dtype=jnp.int32)
    cos_turn, sin_turn = phase_table(index, row_index, length)
    slow = jnp.arange(SPLIT_HI, dtype=jnp.int32)
    fast = jnp.arange(SPLIT_LO, dtype=jnp.int32)
    cos_row, sin_row = phase_table(slow, fast, SPLIT_HI * SPLIT_LO)
    cos_fast, sin_fast = phase_table(fast, fast, SPLIT_LO)
    second_matrix = jnp.concatenate(
        [
            jnp.concatenate([cos_fast, -sin_fast], axis=1),
            jnp.concatenate([sin_fast, cos_fast], axis=1),
        ]
    ) * (1.0 / math.sqrt(SPLIT_HI * SPLIT_LO))
    return (first_matrix, cos_turn, sin_turn), (second_matrix, cos_row, sin_row)


def shards(owners, coefficients, batch_weights, claimed, point_index, point_cycle):
    polys, extent, rows_here = coefficients.shape
    length = extent * rows_here * owners
    first_tables, second_tables = transform_tables(extent, rows_here, length)
    edge = max(1, polys // SHARE)
    counts = (edge, polys - 2 * edge, edge)
    starts = (0, edge, polys - edge)

    def opened(i, tables):
        return first_section(coefficients, tables, starts[i], counts[i], owners)

    def passed(sent):
        return lax.all_to_all(sent, "coef", split_axis=0, concat_axis=0, tiled=True)

    sent, weights = lax.optimization_barrier((opened(0, first_tables), batch_weights))
    received = [passed(sent)]
    combined = combine(weights, coefficients)
    combined_here = lax.psum_scatter(
        combined, ("poly", "limb"), scatter_dimension=0, tiled=True
    )
    received.append(passed(opened(1, first_tables)))
    offsets = jnp.sum(batch_weights[None] * claimed, axis=2)
    offsets_here = lax.psum_scatter(
        offsets, ("poly", "limb"), scatter_dimension=1, tiled=True
    )
    quotient = quotient_section(combined_here, offsets_here, point_index, point_cycle, owners)
    evaluations = second_section(received[0], second_tables, starts[0], polys, None)
    matrix, quotient, evaluations = lax.optimization_barrier(
        (first_tables[0], quotient, evaluations)
    )
    received.append(passed(opened(2, (matrix,) + first_tables[1:])))
    for i in (1, 2):
        evaluations = second_section(received[i], second_tables, starts[i], polys, evaluations)
    return (evaluations, quotient)


def solution(mesh):
    placed = (
        P(("parts", "poly", "limb"), None, "coef"),
        P("parts", ("poly", "limb")),
        P(None, "parts", ("poly", "limb")),
        P(("parts", "poly", "limb")),
        P(("parts", "poly", "limb")),
    )
    return jax.shard_map(
        functools.partial(shards, mesh.shape["coef"]),
        mesh=mesh,
        in_specs=placed,
        out_specs=(
            P(None, "coef", ("parts", "poly", "limb"), None, None),
            P(None, ("parts", "poly", "limb"), None, "coef"),
        ),
        check_vma=False,
    )
```

```python
import functools
import math

import jax
import jax.numpy as jnp
from jax import lax
from jax.experimental import pallas as pl
from jax.experimental.pallas import tpu as pltpu
from jax.sharding import PartitionSpec as P


SPLIT_HI = 32
SPLIT_LO = 128
SHARE = 6

precise = lax.Precision.HIGHEST


def phase_table(row_index, col_index, length):
    product = row_index[:, None] * col_index[None, :] % length
    angles = product.astype(jnp.float32) * (2.0 * math.pi / length)
    return (jnp.cos(angles), jnp.sin(angles))


def cost(flops, moved):
    return pl.CostEstimate(flops=flops, bytes_accessed=moved, transcendentals=0)


def first_kernel(mat_ref, cos_ref, sin_ref, x_ref, out_ref):
    targets, _, _, groups, per_target, lanes = out_ref.shape
    extent = targets * per_target
    for g in range(groups):
        cols = slice(g * lanes, (g + 1) * lanes)
        both = jnp.dot(mat_ref[...], x_ref[0, :, cols], precision=precise,
                       preferred_element_type=jnp.float32)
        real, imag = both[:extent], both[extent:]
        cos_turn, sin_turn = cos_ref[:, cols], sin_ref[:, cols]
        turned_real = real * cos_turn + imag * sin_turn
        turned_imag = imag * cos_turn - real * sin_turn
        for t in range(targets):
            rows = slice(t * per_target, (t + 1) * per_target)
            out_ref[t, 0, 0, g] = turned_real[rows]
            out_ref[t, 0, 1, g] = turned_imag[rows]


def first_section(values, tables, start, count, targets):
    matrix, cos_turn, sin_turn = tables
    _, extent, rows_here = values.shape
    groups = rows_here // SPLIT_LO
    per_target = extent // targets
    shape = (targets, count, 2, groups, per_target, SPLIT_LO)
    block = (targets, 1, 2, groups, per_target, SPLIT_LO)
    size = count * 2 * extent * rows_here
    return pl.pallas_call(
        first_kernel,
        grid=(count,),
        in_specs=[
            pl.BlockSpec((2 * extent, extent), lambda p: (0, 0)),
            pl.BlockSpec((extent, rows_here), lambda p: (0, 0)),
            pl.BlockSpec((extent, rows_here), lambda p: (0, 0)),
            pl.BlockSpec((1, extent, rows_here), lambda p: (start + p, 0, 0)),
        ],
        out_specs=pl.BlockSpec(block, lambda p: (0, p, 0, 0, 0, 0)),
        out_shape=jax.ShapeDtypeStruct(shape, jnp.float32),
        compiler_params=pltpu.CompilerParams(vmem_limit_bytes=60 << 20),
        cost_estimate=cost(size * extent * 12, size * 6),
        name="first_section",
    )(matrix, cos_turn, sin_turn, values)


def fft(pieces):
    count = len(pieces)
    if count == 1:
        return pieces
    even, odd = fft(pieces[0::2]), fft(pieces[1::2])
    low, high = [], []
    for k in range(count // 2):
        er, ei = even[k]
        orr, oi = odd[k]
        if k == 0:
            tr, ti = orr, oi
        elif 4 * k == count:
            tr, ti = oi, -orr
        else:
            c = math.cos(2 * math.pi * k / count)
            s = math.sin(2 * math.pi * k / count)
            if 8 * k == count:
                tr, ti = (orr + oi) * c, (oi - orr) * c
            elif 8 * k == 3 * count:
                tr, ti = (oi - orr) * s, (orr + oi) * (-s)
            else:
                tr, ti = orr * c + oi * s, oi * c - orr * s
        low.append((er + tr, ei + ti))
        high.append((er - tr, ei - ti))
    return low + high


def second_kernel(mat_ref, cos_ref, sin_ref, in_ref, *rest):
    out_ref, real_ref, imag_ref = rest[-3:]
    sources, _, _, groups, here, lanes = in_ref.shape
    pieces = [
        (in_ref[s, 0, 0, g], in_ref[s, 0, 1, g]) for s in range(sources) for g in range(groups)
    ]
    for v, (real, imag) in enumerate(fft(pieces)):
        cos_turn, sin_turn = cos_ref[v : v + 1], sin_ref[v : v + 1]
        at = pl.ds(v, here, stride=SPLIT_HI)
        real_ref[at, :] = real * cos_turn + imag * sin_turn
        imag_ref[at, :] = imag * cos_turn - real * sin_turn
    both = jnp.concatenate([real_ref[...], imag_ref[...]], axis=1)
    done = jnp.dot(both, mat_ref[...], precision=precise, preferred_element_type=jnp.float32)
    out_ref[0, :, 0] = done[:, :lanes].reshape(here, SPLIT_HI, lanes)
    out_ref[1, :, 0] = done[:, lanes:].reshape(here, SPLIT_HI, lanes)


def second_section(received, tables, start, total, held):
    matrix, cos_turn, sin_turn = tables
    sources, count, _, groups, per_target, lanes = received.shape
    here = min(8, per_target)
    out_shape = jax.ShapeDtypeStruct((2, per_target, total, SPLIT_HI, lanes), jnp.float32)
    size = received.size
    operands = [matrix, cos_turn, sin_turn, received]
    in_specs = [
        pl.BlockSpec(matrix.shape, lambda p, k: (0, 0)),
        pl.BlockSpec(cos_turn.shape, lambda p, k: (0, 0)),
        pl.BlockSpec(sin_turn.shape, lambda p, k: (0, 0)),
        pl.BlockSpec((sources, 1, 2, groups, here, lanes), lambda p, k: (0, p, 0, 0, k, 0)),
    ]
    aliases = {}
    if held is not None:
        operands.append(held)
        in_specs.append(pl.BlockSpec(memory_space=pl.ANY))
        aliases = {4: 0}
    return pl.pallas_call(
        second_kernel,
        grid=(count, per_target // here),
        in_specs=in_specs,
        out_specs=pl.BlockSpec(
            (2, here, 1, SPLIT_HI, lanes), lambda p, k: (0, k, start + p, 0, 0)
        ),
        out_shape=out_shape,
        scratch_shapes=[pltpu.VMEM((SPLIT_HI * here, lanes), jnp.float32)] * 2,
        input_output_aliases=aliases,
        compiler_params=pltpu.CompilerParams(vmem_limit_bytes=16 << 20),
        cost_estimate=cost(size * 2 * lanes * 12, size * 8),
        name="second_section",
    )(*operands)


def combine_kernel(weight_ref, x_ref, *out_refs):
    columns, polys = weight_ref.shape
    each = columns // len(out_refs)
    for g in range(x_ref.shape[2] // SPLIT_LO):
        cols = slice(g * SPLIT_LO, (g + 1) * SPLIT_LO)
        rows = [x_ref[p, :, cols] for p in range(polys)]
        for j in range(columns):
            total = rows[0] * weight_ref[j, 0]
            for p in range(1, polys):
                total = total + rows[p] * weight_ref[j, p]
            out_refs[j // each][j % each, :, cols] = total


def combine(weights, values, targets):
    polys, extent, rows_here = values.shape
    columns = weights.shape[0]
    each = columns // targets
    size = extent * rows_here
    return pl.pallas_call(
        combine_kernel,
        grid=(extent // 8,),
        in_specs=[
            pl.BlockSpec(memory_space=pltpu.SMEM),
            pl.BlockSpec((polys, 8, rows_here), lambda n: (0, n, 0)),
        ],
        out_specs=[pl.BlockSpec((each, 8, rows_here), lambda n: (0, n, 0))] * targets,
        out_shape=[jax.ShapeDtypeStruct((each, extent, rows_here), jnp.float32)] * targets,
        compiler_params=pltpu.CompilerParams(vmem_limit_bytes=60 << 20),
        cost_estimate=cost(size * columns * polys * 20, size * 4 * (columns + polys)),
        name="combine",
    )(weights, values)


def column_sums(weights, values):
    axes = ("poly", "limb")
    group = lax.axis_size(axes)
    each = weights.shape[0] // group
    me = lax.axis_index(axes)
    turned = lax.dynamic_slice_in_dim(
        jnp.concatenate([weights, weights]), me * each, weights.shape[0], axis=0
    )
    parts = combine(turned, values, group)
    total = parts[0]
    for step in range(1, group):
        order = [(i, (i + step) % group) for i in range(group)]
        total = total + lax.ppermute(parts[step], axes, order)
    return total


def powers(exponents, point_index, log_radius, length):
    shape = (-1,) + (1,) * exponents.ndim
    phase = (exponents[None] * point_index.reshape(shape)) & (length - 1)
    angles = phase.astype(jnp.float32) * (2.0 * math.pi / length)
    size = jnp.exp(-exponents[None].astype(jnp.float32) * log_radius.reshape(shape))
    return size * jnp.cos(angles), size * jnp.sin(angles)


def quotient_kernel(matrix_ref, step_ref, carry_ref, c_ref, out_ref):
    _, width = c_ref.shape[1:]
    lanes = step_ref.shape[2]
    step_real, step_imag = step_ref[0, 0:1], step_ref[0, 1:2]
    carry = carry_ref[0]
    carry_real, carry_imag = carry[:, 0:1], carry[:, 1:2]
    for g in range(width // lanes):
        cols = slice(g * lanes, (g + 1) * lanes)
        local = jnp.dot(c_ref[0, :, cols], matrix_ref[0], precision=precise,
                        preferred_element_type=jnp.float32)
        real = local[:, :lanes] + (step_real * carry_real - step_imag * carry_imag)
        imag = local[:, lanes:] + (step_real * carry_imag + step_imag * carry_real)
        out_ref[0, 0, :, cols] = real
        out_ref[1, 0, :, cols] = imag
        carry_real, carry_imag = real[:, lanes - 1 :], imag[:, lanes - 1 :]


def quotient_section(combined, offsets, point_index, point_cycle, owners, sent):
    columns, extent, rows_here = combined.shape
    length = extent * rows_here * owners
    lanes = SPLIT_LO
    log_radius = jnp.log1p((point_cycle.astype(jnp.float32) + 1.0) / 512.0)
    power = functools.partial(
        powers, point_index=point_index, log_radius=log_radius, length=length
    )
    index = jnp.arange(lanes, dtype=jnp.int32)
    ahead = index[None, :] - index[:, None] + 1
    below = (ahead > 0)[None]
    local_real, local_imag = power(jnp.maximum(ahead, 0))
    matrix = jnp.concatenate(
        [jnp.where(below, -local_real, 0.0), jnp.where(below, -local_imag, 0.0)], axis=2
    )
    step = jnp.stack(power(index + 1), axis=1)
    end_real, end_imag = power(rows_here - jnp.arange(rows_here, dtype=jnp.int32))
    ends = jnp.stack(
        [
            -jnp.sum(combined * end_real[:, None, :], axis=2),
            -jnp.sum(combined * end_imag[:, None, :], axis=2),
        ]
    )
    ends, sent = lax.optimization_barrier((ends, sent))
    gathered = lax.all_gather(ends, "coef")
    gathered, sent = lax.optimization_barrier((gathered, sent))
    me = lax.axis_index("coef")
    shift = offsets * math.sqrt(length)
    turn_real, turn_imag = power(jnp.full((), rows_here, jnp.int32))
    first = jnp.stack(
        [
            turn_real * shift[0] - turn_imag * shift[1],
            turn_real * shift[1] + turn_imag * shift[0],
        ]
    )
    gathered = gathered.at[0, :, :, 0].add(first)
    row = jnp.arange(extent, dtype=jnp.int32)
    owner = jnp.arange(owners, dtype=jnp.int32)
    segments = extent * owners
    away = (
        (row[:, None, None] * owners + me)
        - (row[None, None, :] * owners + owner[None, :, None])
        - 1
        + segments
    ) % segments
    pass_real, pass_imag = power(away * rows_here)
    whole = 1.0 - power(jnp.full((), length, jnp.int32))[0]
    ends_real = jnp.transpose(gathered[:, 0], (1, 0, 2))[:, None]
    ends_imag = jnp.transpose(gathered[:, 1], (1, 0, 2))[:, None]
    carry_real = jnp.sum(pass_real * ends_real - pass_imag * ends_imag, axis=(2, 3))
    carry_imag = jnp.sum(pass_real * ends_imag + pass_imag * ends_real, axis=(2, 3))
    carry = jnp.stack([carry_real, carry_imag], axis=2) / whole[:, None, None]
    starts = ((row == 0) & (me == 0))[None, :, None]
    carry = carry + jnp.where(starts, shift.T[:, None, :], 0.0)
    size = columns * extent * rows_here
    call = pl.pallas_call(
        quotient_kernel,
        grid=(columns,),
        in_specs=[
            pl.BlockSpec((1, lanes, 2 * lanes), lambda j: (j, 0, 0)),
            pl.BlockSpec((1, 2, lanes), lambda j: (j, 0, 0)),
            pl.BlockSpec((1, extent, 2), lambda j: (j, 0, 0)),
            pl.BlockSpec((1, extent, rows_here), lambda j: (j, 0, 0)),
        ],
        out_specs=pl.BlockSpec((2, 1, extent, rows_here), lambda j: (0, j, 0, 0)),
        out_shape=jax.ShapeDtypeStruct((2, columns, extent, rows_here), jnp.float32),
        compiler_params=pltpu.CompilerParams(vmem_limit_bytes=16 << 20),
        cost_estimate=cost(size * 4 * lanes * 6, size * 12),
        name="quotient",
    )
    return call(matrix, step, carry, combined), sent


def transform_tables(extent, rows_here, length):
    index = jnp.arange(extent, dtype=jnp.int32)
    cos_table, sin_table = phase_table(index, index, extent)
    first_matrix = jnp.concatenate([cos_table, -sin_table]) * (1.0 / math.sqrt(extent))
    row_index = lax.axis_index("coef") * rows_here + jnp.arange(rows_here, dtype=jnp.int32)
    cos_turn, sin_turn = phase_table(index, row_index, length)
    slow = jnp.arange(SPLIT_HI, dtype=jnp.int32)
    fast = jnp.arange(SPLIT_LO, dtype=jnp.int32)
    cos_row, sin_row = phase_table(slow, fast, SPLIT_HI * SPLIT_LO)
    cos_fast, sin_fast = phase_table(fast, fast, SPLIT_LO)
    second_matrix = jnp.concatenate(
        [
            jnp.concatenate([cos_fast, -sin_fast], axis=1),
            jnp.concatenate([sin_fast, cos_fast], axis=1),
        ]
    ) * (1.0 / math.sqrt(SPLIT_HI * SPLIT_LO))
    return (first_matrix, cos_turn, sin_turn), (second_matrix, cos_row, sin_row)


def shards(owners, coefficients, batch_weights, claimed, point_index, point_cycle):
    polys, extent, rows_here = coefficients.shape
    length = extent * rows_here * owners
    first_tables, second_tables = transform_tables(extent, rows_here, length)
    edge = max(1, polys // SHARE)
    counts = (edge, polys - 2 * edge, edge)
    starts = (0, edge, polys - edge)

    def opened(i):
        return first_section(coefficients, first_tables, starts[i], counts[i], owners)

    def passed(sent):
        return lax.all_to_all(sent, "coef", split_axis=0, concat_axis=0, tiled=True)

    received = [passed(opened(0))]
    combined_here = column_sums(batch_weights, coefficients)
    received.append(passed(opened(1)))
    offsets = jnp.sum(batch_weights[None] * claimed, axis=2)
    offsets_here = lax.psum_scatter(
        offsets, ("poly", "limb"), scatter_dimension=1, tiled=True
    )
    quotient, sent = quotient_section(
        combined_here, offsets_here, point_index, point_cycle, owners, opened(2)
    )
    received.append(passed(sent))
    evaluations = second_section(received[0], second_tables, starts[0], polys, None)
    for i in (1, 2):
        evaluations = second_section(
            received[i], second_tables, starts[i], polys, evaluations
        )
    return (evaluations, quotient)


def solution(mesh):
    placed = (
        P(("parts", "poly", "limb"), None, "coef"),
        P("parts", ("poly", "limb")),
        P(None, "parts", ("poly", "limb")),
        P(("parts", "poly", "limb")),
        P(("parts", "poly", "limb")),
    )
    return jax.shard_map(
        functools.partial(shards, mesh.shape["coef"]),
        mesh=mesh,
        in_specs=placed,
        out_specs=(
            P(None, "coef", ("parts", "poly", "limb"), None, None),
            P(None, ("parts", "poly", "limb"), None, "coef"),
        ),
        check_vma=False,
    )
```

```python
import functools
import math

import jax
import jax.numpy as jnp
from jax import lax
from jax.experimental import pallas as pl
from jax.experimental.pallas import tpu as pltpu
from jax.sharding import PartitionSpec as P


SPLIT_HI = 32
SPLIT_LO = 128
SHARE = 6

precise = lax.Precision.HIGHEST


def phase_table(row_index, col_index, length):
    product = row_index[:, None] * col_index[None, :] % length
    angles = product.astype(jnp.float32) * (2.0 * math.pi / length)
    return (jnp.cos(angles), jnp.sin(angles))


def cost(flops, moved):
    return pl.CostEstimate(flops=flops, bytes_accessed=moved, transcendentals=0)


def first_kernel(mat_ref, cos_ref, sin_ref, x_ref, out_ref):
    targets, _, _, groups, per_target, lanes = out_ref.shape
    extent = targets * per_target
    for g in range(groups):
        cols = slice(g * lanes, (g + 1) * lanes)
        both = jnp.dot(mat_ref[...], x_ref[0, :, cols], precision=precise,
                       preferred_element_type=jnp.float32)
        real, imag = both[:extent], both[extent:]
        cos_turn, sin_turn = cos_ref[:, cols], sin_ref[:, cols]
        turned_real = real * cos_turn + imag * sin_turn
        turned_imag = imag * cos_turn - real * sin_turn
        for t in range(targets):
            rows = slice(t * per_target, (t + 1) * per_target)
            out_ref[t, 0, 0, g] = turned_real[rows]
            out_ref[t, 0, 1, g] = turned_imag[rows]


def first_section(values, tables, start, count, targets):
    matrix, cos_turn, sin_turn = tables
    _, extent, rows_here = values.shape
    groups = rows_here // SPLIT_LO
    per_target = extent // targets
    shape = (targets, count, 2, groups, per_target, SPLIT_LO)
    block = (targets, 1, 2, groups, per_target, SPLIT_LO)
    size = count * 2 * extent * rows_here
    return pl.pallas_call(
        first_kernel,
        grid=(count,),
        in_specs=[
            pl.BlockSpec((2 * extent, extent), lambda p: (0, 0)),
            pl.BlockSpec((extent, rows_here), lambda p: (0, 0)),
            pl.BlockSpec((extent, rows_here), lambda p: (0, 0)),
            pl.BlockSpec((1, extent, rows_here), lambda p: (start + p, 0, 0)),
        ],
        out_specs=pl.BlockSpec(block, lambda p: (0, p, 0, 0, 0, 0)),
        out_shape=jax.ShapeDtypeStruct(shape, jnp.float32),
        compiler_params=pltpu.CompilerParams(vmem_limit_bytes=60 << 20),
        cost_estimate=cost(size * extent * 12, size * 6),
        name="first_section",
    )(matrix, cos_turn, sin_turn, values)


def fft(pieces):
    count = len(pieces)
    if count == 1:
        return pieces
    even, odd = fft(pieces[0::2]), fft(pieces[1::2])
    low, high = [], []
    for k in range(count // 2):
        er, ei = even[k]
        orr, oi = odd[k]
        if k == 0:
            tr, ti = orr, oi
        elif 4 * k == count:
            tr, ti = oi, -orr
        else:
            c = math.cos(2 * math.pi * k / count)
            s = math.sin(2 * math.pi * k / count)
            if 8 * k == count:
                tr, ti = (orr + oi) * c, (oi - orr) * c
            elif 8 * k == 3 * count:
                tr, ti = (oi - orr) * s, (orr + oi) * (-s)
            else:
                tr, ti = orr * c + oi * s, oi * c - orr * s
        low.append((er + tr, ei + ti))
        high.append((er - tr, ei - ti))
    return low + high


def second_kernel(mat_ref, cos_ref, sin_ref, in_ref, *rest):
    out_ref, real_ref, imag_ref = rest[-3:]
    sources, _, _, groups, here, lanes = in_ref.shape
    pieces = [
        (in_ref[s, 0, 0, g], in_ref[s, 0, 1, g]) for s in range(sources) for g in range(groups)
    ]
    for v, (real, imag) in enumerate(fft(pieces)):
        cos_turn, sin_turn = cos_ref[v : v + 1], sin_ref[v : v + 1]
        at = pl.ds(v, here, stride=SPLIT_HI)
        real_ref[at, :] = real * cos_turn + imag * sin_turn
        imag_ref[at, :] = imag * cos_turn - real * sin_turn
    both = jnp.concatenate([real_ref[...], imag_ref[...]], axis=1)
    done = jnp.dot(both, mat_ref[...], precision=precise, preferred_element_type=jnp.float32)
    out_ref[0, :, 0] = done[:, :lanes].reshape(here, SPLIT_HI, lanes)
    out_ref[1, :, 0] = done[:, lanes:].reshape(here, SPLIT_HI, lanes)


def second_section(received, tables, start, total, held):
    matrix, cos_turn, sin_turn = tables
    sources, count, _, groups, per_target, lanes = received.shape
    here = min(8, per_target)
    out_shape = jax.ShapeDtypeStruct((2, per_target, total, SPLIT_HI, lanes), jnp.float32)
    size = received.size
    operands = [matrix, cos_turn, sin_turn, received]
    in_specs = [
        pl.BlockSpec(matrix.shape, lambda p, k: (0, 0)),
        pl.BlockSpec(cos_turn.shape, lambda p, k: (0, 0)),
        pl.BlockSpec(sin_turn.shape, lambda p, k: (0, 0)),
        pl.BlockSpec((sources, 1, 2, groups, here, lanes), lambda p, k: (0, p, 0, 0, k, 0)),
    ]
    aliases = {}
    if held is not None:
        operands.append(held)
        in_specs.append(pl.BlockSpec(memory_space=pl.ANY))
        aliases = {4: 0}
    return pl.pallas_call(
        second_kernel,
        grid=(count, per_target // here),
        in_specs=in_specs,
        out_specs=pl.BlockSpec(
            (2, here, 1, SPLIT_HI, lanes), lambda p, k: (0, k, start + p, 0, 0)
        ),
        out_shape=out_shape,
        scratch_shapes=[pltpu.VMEM((SPLIT_HI * here, lanes), jnp.float32)] * 2,
        input_output_aliases=aliases,
        compiler_params=pltpu.CompilerParams(vmem_limit_bytes=16 << 20),
        cost_estimate=cost(size * 2 * lanes * 12, size * 8),
        name="second_section",
    )(*operands)


def combine_kernel(weight_ref, x_ref, *out_refs):
    columns, polys = weight_ref.shape
    each = columns // len(out_refs)
    for g in range(x_ref.shape[2] // SPLIT_LO):
        cols = slice(g * SPLIT_LO, (g + 1) * SPLIT_LO)
        rows = [x_ref[p, :, cols] for p in range(polys)]
        for j in range(columns):
            total = rows[0] * weight_ref[j, 0]
            for p in range(1, polys):
                total = total + rows[p] * weight_ref[j, p]
            out_refs[j // each][j % each, :, cols] = total


def combine(weights, values, targets):
    polys, extent, rows_here = values.shape
    columns = weights.shape[0]
    each = columns // targets
    size = extent * rows_here
    return pl.pallas_call(
        combine_kernel,
        grid=(extent // 8,),
        in_specs=[
            pl.BlockSpec(memory_space=pltpu.SMEM),
            pl.BlockSpec((polys, 8, rows_here), lambda n: (0, n, 0)),
        ],
        out_specs=[pl.BlockSpec((each, 8, rows_here), lambda n: (0, n, 0))] * targets,
        out_shape=[jax.ShapeDtypeStruct((each, extent, rows_here), jnp.float32)] * targets,
        compiler_params=pltpu.CompilerParams(vmem_limit_bytes=60 << 20),
        cost_estimate=cost(size * columns * polys * 20, size * 4 * (columns + polys)),
        name="combine",
    )(weights, values)


def column_sums(weights, values):
    axes = ("poly", "limb")
    group = lax.axis_size(axes)
    each = weights.shape[0] // group
    me = lax.axis_index(axes)
    turned = lax.dynamic_slice_in_dim(
        jnp.concatenate([weights, weights]), me * each, weights.shape[0], axis=0
    )
    parts = combine(turned, values, group)
    total = parts[0]
    for step in range(1, group):
        order = [(i, (i + step) % group) for i in range(group)]
        total = total + lax.ppermute(parts[step], axes, order)
    return total


def powers(exponents, point_index, log_radius, length):
    shape = (-1,) + (1,) * exponents.ndim
    phase = (exponents[None] * point_index.reshape(shape)) & (length - 1)
    angles = phase.astype(jnp.float32) * (2.0 * math.pi / length)
    size = jnp.exp(-exponents[None].astype(jnp.float32) * log_radius.reshape(shape))
    return size * jnp.cos(angles), size * jnp.sin(angles)


def quotient_kernel(matrix_ref, step_ref, carry_ref, c_ref, out_ref):
    _, width = c_ref.shape[1:]
    lanes = step_ref.shape[2]
    step_real, step_imag = step_ref[0, 0:1], step_ref[0, 1:2]
    carry = carry_ref[0]
    carry_real, carry_imag = carry[:, 0:1], carry[:, 1:2]
    for g in range(width // lanes):
        cols = slice(g * lanes, (g + 1) * lanes)
        local = jnp.dot(c_ref[0, :, cols], matrix_ref[0], precision=precise,
                        preferred_element_type=jnp.float32)
        real = local[:, :lanes] + (step_real * carry_real - step_imag * carry_imag)
        imag = local[:, lanes:] + (step_real * carry_imag + step_imag * carry_real)
        out_ref[0, 0, :, cols] = real
        out_ref[1, 0, :, cols] = imag
        carry_real, carry_imag = real[:, lanes - 1 :], imag[:, lanes - 1 :]


def shared(ends, owners):
    me = lax.axis_index("coef")
    if owners > 8:
        return lax.all_gather(ends, "coef"), jnp.arange(owners, dtype=jnp.int32)
    arrived = [ends]
    for step in range(1, owners):
        order = [(i, (i + step) % owners) for i in range(owners)]
        arrived.append(lax.ppermute(ends, "coef", order))
    return jnp.stack(arrived), (me - jnp.arange(owners, dtype=jnp.int32)) % owners


def quotient_section(combined, offsets, point_index, point_cycle, owners):
    columns, extent, rows_here = combined.shape
    length = extent * rows_here * owners
    lanes = SPLIT_LO
    log_radius = jnp.log1p((point_cycle.astype(jnp.float32) + 1.0) / 512.0)
    power = functools.partial(
        powers, point_index=point_index, log_radius=log_radius, length=length
    )
    index = jnp.arange(lanes, dtype=jnp.int32)
    ahead = index[None, :] - index[:, None] + 1
    below = (ahead > 0)[None]
    local_real, local_imag = power(jnp.maximum(ahead, 0))
    matrix = jnp.concatenate(
        [jnp.where(below, -local_real, 0.0), jnp.where(below, -local_imag, 0.0)], axis=2
    )
    step = jnp.stack(power(index + 1), axis=1)
    end_real, end_imag = power(rows_here - jnp.arange(rows_here, dtype=jnp.int32))
    ends = jnp.stack(
        [
            -jnp.sum(combined * end_real[:, None, :], axis=2),
            -jnp.sum(combined * end_imag[:, None, :], axis=2),
        ]
    )
    me = lax.axis_index("coef")
    gathered, owner = shared(ends, owners)
    shift = offsets * math.sqrt(length)
    turn_real, turn_imag = power(jnp.full((), rows_here, jnp.int32))
    first = jnp.stack(
        [
            turn_real * shift[0] - turn_imag * shift[1],
            turn_real * shift[1] + turn_imag * shift[0],
        ]
    )
    row = jnp.arange(extent, dtype=jnp.int32)
    opening = (owner[:, None] == 0) & (row[None, :] == 0)
    gathered = gathered + jnp.where(
        opening[:, None, None, :], first[None, :, :, None], 0.0
    )
    segments = extent * owners
    away = (
        (row[:, None, None] * owners + me)
        - (row[None, None, :] * owners + owner[None, :, None])
        - 1
        + segments
    ) % segments
    pass_real, pass_imag = power(away * rows_here)
    whole = 1.0 - power(jnp.full((), length, jnp.int32))[0]
    ends_real = jnp.transpose(gathered[:, 0], (1, 0, 2))[:, None]
    ends_imag = jnp.transpose(gathered[:, 1], (1, 0, 2))[:, None]
    carry_real = jnp.sum(pass_real * ends_real - pass_imag * ends_imag, axis=(2, 3))
    carry_imag = jnp.sum(pass_real * ends_imag + pass_imag * ends_real, axis=(2, 3))
    carry = jnp.stack([carry_real, carry_imag], axis=2) / whole[:, None, None]
    starts = ((row == 0) & (me == 0))[None, :, None]
    carry = carry + jnp.where(starts, shift.T[:, None, :], 0.0)
    size = columns * extent * rows_here
    return pl.pallas_call(
        quotient_kernel,
        grid=(columns,),
        in_specs=[
            pl.BlockSpec((1, lanes, 2 * lanes), lambda j: (j, 0, 0)),
            pl.BlockSpec((1, 2, lanes), lambda j: (j, 0, 0)),
            pl.BlockSpec((1, extent, 2), lambda j: (j, 0, 0)),
            pl.BlockSpec((1, extent, rows_here), lambda j: (j, 0, 0)),
        ],
        out_specs=pl.BlockSpec((2, 1, extent, rows_here), lambda j: (0, j, 0, 0)),
        out_shape=jax.ShapeDtypeStruct((2, columns, extent, rows_here), jnp.float32),
        compiler_params=pltpu.CompilerParams(vmem_limit_bytes=16 << 20),
        cost_estimate=cost(size * 4 * lanes * 6, size * 12),
        name="quotient",
    )(matrix, step, carry, combined)


def transform_tables(extent, rows_here, length):
    index = jnp.arange(extent, dtype=jnp.int32)
    cos_table, sin_table = phase_table(index, index, extent)
    first_matrix = jnp.concatenate([cos_table, -sin_table]) * (1.0 / math.sqrt(extent))
    row_index = lax.axis_index("coef") * rows_here + jnp.arange(rows_here, dtype=jnp.int32)
    cos_turn, sin_turn = phase_table(index, row_index, length)
    slow = jnp.arange(SPLIT_HI, dtype=jnp.int32)
    fast = jnp.arange(SPLIT_LO, dtype=jnp.int32)
    cos_row, sin_row = phase_table(slow, fast, SPLIT_HI * SPLIT_LO)
    cos_fast, sin_fast = phase_table(fast, fast, SPLIT_LO)
    second_matrix = jnp.concatenate(
        [
            jnp.concatenate([cos_fast, -sin_fast], axis=1),
            jnp.concatenate([sin_fast, cos_fast], axis=1),
        ]
    ) * (1.0 / math.sqrt(SPLIT_HI * SPLIT_LO))
    return (first_matrix, cos_turn, sin_turn), (second_matrix, cos_row, sin_row)


def shards(owners, coefficients, batch_weights, claimed, point_index, point_cycle):
    polys, extent, rows_here = coefficients.shape
    length = extent * rows_here * owners
    first_tables, second_tables = transform_tables(extent, rows_here, length)
    edge = max(1, polys // SHARE)
    head = max(1, edge // 2)
    counts = (head, polys - head - edge, edge)
    starts = (0, head, polys - edge)

    def opened(i):
        return first_section(coefficients, first_tables, starts[i], counts[i], owners)

    def passed(sent):
        return lax.all_to_all(sent, "coef", split_axis=0, concat_axis=0, tiled=True)

    received = [passed(opened(0))]
    combined_here = column_sums(batch_weights, coefficients)
    received.append(passed(opened(1)))
    offsets = jnp.sum(batch_weights[None] * claimed, axis=2)
    offsets_here = lax.psum_scatter(
        offsets, ("poly", "limb"), scatter_dimension=1, tiled=True
    )
    quotient = quotient_section(
        combined_here, offsets_here, point_index, point_cycle, owners
    )
    received.append(passed(opened(2)))
    evaluations = second_section(received[0], second_tables, starts[0], polys, None)
    for i in (1, 2):
        evaluations = second_section(
            received[i], second_tables, starts[i], polys, evaluations
        )
    return (evaluations, quotient)


def solution(mesh):
    placed = (
        P(("parts", "poly", "limb"), None, "coef"),
        P("parts", ("poly", "limb")),
        P(None, "parts", ("poly", "limb")),
        P(("parts", "poly", "limb")),
        P(("parts", "poly", "limb")),
    )
    return jax.shard_map(
        functools.partial(shards, mesh.shape["coef"]),
        mesh=mesh,
        in_specs=placed,
        out_specs=(
            P(None, "coef", ("parts", "poly", "limb"), None, None),
            P(None, ("parts", "poly", "limb"), None, "coef"),
        ),
        check_vma=False,
    )
```

```python
import functools
import math

import jax
import jax.numpy as jnp
from jax import lax
from jax.experimental import pallas as pl
from jax.experimental.pallas import tpu as pltpu
from jax.sharding import PartitionSpec as P


SPLIT_HI = 32
SPLIT_LO = 128
SHARE = 6

precise = lax.Precision.HIGHEST


def phase_table(row_index, col_index, length):
    product = row_index[:, None] * col_index[None, :] % length
    angles = product.astype(jnp.float32) * (2.0 * math.pi / length)
    return (jnp.cos(angles), jnp.sin(angles))


def cost(flops, moved):
    return pl.CostEstimate(flops=flops, bytes_accessed=moved, transcendentals=0)


def first_kernel(mat_ref, cos_ref, sin_ref, x_ref, *out_refs):
    targets = len(out_refs)
    _, _, groups, per_target, lanes = out_refs[0].shape
    extent = targets * per_target
    for g in range(groups):
        cols = slice(g * lanes, (g + 1) * lanes)
        both = jnp.dot(mat_ref[...], x_ref[0, :, cols], precision=precise,
                       preferred_element_type=jnp.float32)
        real, imag = both[:extent], both[extent:]
        cos_turn, sin_turn = cos_ref[:, cols], sin_ref[:, cols]
        turned_real = real * cos_turn + imag * sin_turn
        turned_imag = imag * cos_turn - real * sin_turn
        for t in range(targets):
            rows = slice(t * per_target, (t + 1) * per_target)
            out_refs[t][0, 0, g] = turned_real[rows]
            out_refs[t][0, 1, g] = turned_imag[rows]


def first_section(values, tables, start, count, targets):
    matrix, cos_turn, sin_turn = tables
    _, extent, rows_here = values.shape
    groups = rows_here // SPLIT_LO
    per_target = extent // targets
    shape = (count, 2, groups, per_target, SPLIT_LO)
    block = (1, 2, groups, per_target, SPLIT_LO)
    size = count * 2 * extent * rows_here
    return pl.pallas_call(
        first_kernel,
        grid=(count,),
        in_specs=[
            pl.BlockSpec((2 * extent, extent), lambda p: (0, 0)),
            pl.BlockSpec((extent, rows_here), lambda p: (0, 0)),
            pl.BlockSpec((extent, rows_here), lambda p: (0, 0)),
            pl.BlockSpec((1, extent, rows_here), lambda p: (start + p, 0, 0)),
        ],
        out_specs=[pl.BlockSpec(block, lambda p: (p, 0, 0, 0, 0))] * targets,
        out_shape=[jax.ShapeDtypeStruct(shape, jnp.float32)] * targets,
        compiler_params=pltpu.CompilerParams(vmem_limit_bytes=60 << 20),
        cost_estimate=cost(size * extent * 12, size * 6),
        name="first_section",
    )(matrix, cos_turn, sin_turn, values)


def fft(pieces):
    count = len(pieces)
    if count == 1:
        return pieces
    even, odd = fft(pieces[0::2]), fft(pieces[1::2])
    low, high = [], []
    for k in range(count // 2):
        er, ei = even[k]
        orr, oi = odd[k]
        if k == 0:
            tr, ti = orr, oi
        elif 4 * k == count:
            tr, ti = oi, -orr
        else:
            c = math.cos(2 * math.pi * k / count)
            s = math.sin(2 * math.pi * k / count)
            if 8 * k == count:
                tr, ti = (orr + oi) * c, (oi - orr) * c
            elif 8 * k == 3 * count:
                tr, ti = (oi - orr) * s, (orr + oi) * (-s)
            else:
                tr, ti = orr * c + oi * s, oi * c - orr * s
        low.append((er + tr, ei + ti))
        high.append((er - tr, ei - ti))
    return low + high


def second_kernel(sources, mat_ref, cos_ref, sin_ref, *rest):
    out_ref, real_ref, imag_ref = rest[-3:]
    _, _, groups, here, lanes = rest[0].shape
    in_refs = [rest[-s % sources] for s in range(sources)]
    pieces = [(ref[0, 0, g], ref[0, 1, g]) for ref in in_refs for g in range(groups)]
    for v, (real, imag) in enumerate(fft(pieces)):
        cos_turn, sin_turn = cos_ref[v : v + 1], sin_ref[v : v + 1]
        at = pl.ds(v, here, stride=SPLIT_HI)
        real_ref[at, :] = real * cos_turn + imag * sin_turn
        imag_ref[at, :] = imag * cos_turn - real * sin_turn
    both = jnp.concatenate([real_ref[...], imag_ref[...]], axis=1)
    done = jnp.dot(both, mat_ref[...], precision=precise, preferred_element_type=jnp.float32)
    out_ref[0, :, 0] = done[:, :lanes].reshape(here, SPLIT_HI, lanes)
    out_ref[1, :, 0] = done[:, lanes:].reshape(here, SPLIT_HI, lanes)


def second_section(received, tables, start, total, held):
    matrix, cos_turn, sin_turn = tables
    sources = len(received)
    count, _, groups, per_target, lanes = received[0].shape
    here = min(8, per_target)
    out_shape = jax.ShapeDtypeStruct((2, per_target, total, SPLIT_HI, lanes), jnp.float32)
    size = sources * received[0].size
    operands = [matrix, cos_turn, sin_turn, *received]
    in_specs = [
        pl.BlockSpec(matrix.shape, lambda p, k: (0, 0)),
        pl.BlockSpec(cos_turn.shape, lambda p, k: (0, 0)),
        pl.BlockSpec(sin_turn.shape, lambda p, k: (0, 0)),
    ] + [pl.BlockSpec((1, 2, groups, here, lanes), lambda p, k: (p, 0, 0, k, 0))] * sources
    aliases = {}
    if held is not None:
        operands.append(held)
        in_specs.append(pl.BlockSpec(memory_space=pl.ANY))
        aliases = {3 + sources: 0}
    return pl.pallas_call(
        functools.partial(second_kernel, sources),
        grid=(count, per_target // here),
        in_specs=in_specs,
        out_specs=pl.BlockSpec(
            (2, here, 1, SPLIT_HI, lanes), lambda p, k: (0, k, start + p, 0, 0)
        ),
        out_shape=out_shape,
        scratch_shapes=[pltpu.VMEM((SPLIT_HI * here, lanes), jnp.float32)] * 2,
        input_output_aliases=aliases,
        compiler_params=pltpu.CompilerParams(vmem_limit_bytes=16 << 20),
        cost_estimate=cost(size * 2 * lanes * 12, size * 8),
        name="second_section",
    )(*operands)


def combine_kernel(weight_ref, x_ref, *out_refs):
    columns, polys = weight_ref.shape
    each = columns // len(out_refs)
    for g in range(x_ref.shape[2] // SPLIT_LO):
        cols = slice(g * SPLIT_LO, (g + 1) * SPLIT_LO)
        rows = [x_ref[p, :, cols] for p in range(polys)]
        for j in range(columns):
            total = rows[0] * weight_ref[j, 0]
            for p in range(1, polys):
                total = total + rows[p] * weight_ref[j, p]
            out_refs[j // each][j % each, :, cols] = total


def combine(weights, values, targets):
    polys, extent, rows_here = values.shape
    columns = weights.shape[0]
    each = columns // targets
    size = extent * rows_here
    return pl.pallas_call(
        combine_kernel,
        grid=(extent // 8,),
        in_specs=[
            pl.BlockSpec(memory_space=pltpu.SMEM),
            pl.BlockSpec((polys, 8, rows_here), lambda n: (0, n, 0)),
        ],
        out_specs=[pl.BlockSpec((each, 8, rows_here), lambda n: (0, n, 0))] * targets,
        out_shape=[jax.ShapeDtypeStruct((each, extent, rows_here), jnp.float32)] * targets,
        compiler_params=pltpu.CompilerParams(vmem_limit_bytes=60 << 20),
        cost_estimate=cost(size * columns * polys * 20, size * 4 * (columns + polys)),
        name="combine",
    )(weights, values)


def column_sums(weights, values):
    axes = ("poly", "limb")
    group = lax.axis_size(axes)
    each = weights.shape[0] // group
    me = lax.axis_index(axes)
    turned = lax.dynamic_slice_in_dim(
        jnp.concatenate([weights, weights]), me * each, weights.shape[0], axis=0
    )
    parts = combine(turned, values, group)
    total = parts[0]
    for step in range(1, group):
        order = [(i, (i + step) % group) for i in range(group)]
        total = total + lax.ppermute(parts[step], axes, order)
    return total


def powers(exponents, point_index, log_radius, length):
    shape = (-1,) + (1,) * exponents.ndim
    phase = (exponents[None] * point_index.reshape(shape)) & (length - 1)
    angles = phase.astype(jnp.float32) * (2.0 * math.pi / length)
    size = jnp.exp(-exponents[None].astype(jnp.float32) * log_radius.reshape(shape))
    return size * jnp.cos(angles), size * jnp.sin(angles)


def quotient_kernel(matrix_ref, step_ref, carry_ref, c_ref, out_ref):
    _, width = c_ref.shape[1:]
    lanes = step_ref.shape[2]
    step_real, step_imag = step_ref[0, 0:1], step_ref[0, 1:2]
    carry = carry_ref[0]
    carry_real, carry_imag = carry[:, 0:1], carry[:, 1:2]
    for g in range(width // lanes):
        cols = slice(g * lanes, (g + 1) * lanes)
        local = jnp.dot(c_ref[0, :, cols], matrix_ref[0], precision=precise,
                        preferred_element_type=jnp.float32)
        real = local[:, :lanes] + (step_real * carry_real - step_imag * carry_imag)
        imag = local[:, lanes:] + (step_real * carry_imag + step_imag * carry_real)
        out_ref[0, 0, :, cols] = real
        out_ref[1, 0, :, cols] = imag
        carry_real, carry_imag = real[:, lanes - 1 :], imag[:, lanes - 1 :]


def shared(ends, owners):
    me = lax.axis_index("coef")
    if owners > 8:
        return lax.all_gather(ends, "coef"), jnp.arange(owners, dtype=jnp.int32)
    arrived = [ends]
    for step in range(1, owners):
        order = [(i, (i + step) % owners) for i in range(owners)]
        arrived.append(lax.ppermute(ends, "coef", order))
    return jnp.stack(arrived), (me - jnp.arange(owners, dtype=jnp.int32)) % owners


def quotient_section(combined, offsets, point_index, point_cycle, owners):
    columns, extent, rows_here = combined.shape
    length = extent * rows_here * owners
    lanes = SPLIT_LO
    log_radius = jnp.log1p((point_cycle.astype(jnp.float32) + 1.0) / 512.0)
    power = functools.partial(
        powers, point_index=point_index, log_radius=log_radius, length=length
    )
    index = jnp.arange(lanes, dtype=jnp.int32)
    ahead = index[None, :] - index[:, None] + 1
    below = (ahead > 0)[None]
    local_real, local_imag = power(jnp.maximum(ahead, 0))
    matrix = jnp.concatenate(
        [jnp.where(below, -local_real, 0.0), jnp.where(below, -local_imag, 0.0)], axis=2
    )
    step = jnp.stack(power(index + 1), axis=1)
    end_real, end_imag = power(rows_here - jnp.arange(rows_here, dtype=jnp.int32))
    ends = jnp.stack(
        [
            -jnp.sum(combined * end_real[:, None, :], axis=2),
            -jnp.sum(combined * end_imag[:, None, :], axis=2),
        ]
    )
    me = lax.axis_index("coef")
    gathered, owner = shared(ends, owners)
    shift = offsets * math.sqrt(length)
    turn_real, turn_imag = power(jnp.full((), rows_here, jnp.int32))
    first = jnp.stack(
        [
            turn_real * shift[0] - turn_imag * shift[1],
            turn_real * shift[1] + turn_imag * shift[0],
        ]
    )
    row = jnp.arange(extent, dtype=jnp.int32)
    opening = (owner[:, None] == 0) & (row[None, :] == 0)
    gathered = gathered + jnp.where(
        opening[:, None, None, :], first[None, :, :, None], 0.0
    )
    segments = extent * owners
    away = (
        (row[:, None, None] * owners + me)
        - (row[None, None, :] * owners + owner[None, :, None])
        - 1
        + segments
    ) % segments
    pass_real, pass_imag = power(away * rows_here)
    whole = 1.0 - power(jnp.full((), length, jnp.int32))[0]
    ends_real = jnp.transpose(gathered[:, 0], (1, 0, 2))[:, None]
    ends_imag = jnp.transpose(gathered[:, 1], (1, 0, 2))[:, None]
    carry_real = jnp.sum(pass_real * ends_real - pass_imag * ends_imag, axis=(2, 3))
    carry_imag = jnp.sum(pass_real * ends_imag + pass_imag * ends_real, axis=(2, 3))
    carry = jnp.stack([carry_real, carry_imag], axis=2) / whole[:, None, None]
    starts = ((row == 0) & (me == 0))[None, :, None]
    carry = carry + jnp.where(starts, shift.T[:, None, :], 0.0)
    size = columns * extent * rows_here
    return pl.pallas_call(
        quotient_kernel,
        grid=(columns,),
        in_specs=[
            pl.BlockSpec((1, lanes, 2 * lanes), lambda j: (j, 0, 0)),
            pl.BlockSpec((1, 2, lanes), lambda j: (j, 0, 0)),
            pl.BlockSpec((1, extent, 2), lambda j: (j, 0, 0)),
            pl.BlockSpec((1, extent, rows_here), lambda j: (j, 0, 0)),
        ],
        out_specs=pl.BlockSpec((2, 1, extent, rows_here), lambda j: (0, j, 0, 0)),
        out_shape=jax.ShapeDtypeStruct((2, columns, extent, rows_here), jnp.float32),
        compiler_params=pltpu.CompilerParams(vmem_limit_bytes=16 << 20),
        cost_estimate=cost(size * 4 * lanes * 6, size * 12),
        name="quotient",
    )(matrix, step, carry, combined)


def transform_tables(extent, rows_here, length, owners):
    index = jnp.arange(extent, dtype=jnp.int32)
    me = lax.axis_index("coef")
    turned = (index + me * (extent // owners)) % extent
    cos_table, sin_table = phase_table(turned, index, extent)
    first_matrix = jnp.concatenate([cos_table, -sin_table]) * (1.0 / math.sqrt(extent))
    row_index = me * rows_here + jnp.arange(rows_here, dtype=jnp.int32)
    cos_turn, sin_turn = phase_table(turned, row_index, length)
    slow = jnp.arange(SPLIT_HI, dtype=jnp.int32)
    fast = jnp.arange(SPLIT_LO, dtype=jnp.int32)
    cos_row, sin_row = phase_table(slow, fast + me * rows_here, SPLIT_HI * SPLIT_LO)
    cos_fast, sin_fast = phase_table(fast, fast, SPLIT_LO)
    second_matrix = jnp.concatenate(
        [
            jnp.concatenate([cos_fast, -sin_fast], axis=1),
            jnp.concatenate([sin_fast, cos_fast], axis=1),
        ]
    ) * (1.0 / math.sqrt(SPLIT_HI * SPLIT_LO))
    return (first_matrix, cos_turn, sin_turn), (second_matrix, cos_row, sin_row)


def shards(owners, coefficients, batch_weights, claimed, point_index, point_cycle):
    polys, extent, rows_here = coefficients.shape
    length = extent * rows_here * owners
    first_tables, second_tables = transform_tables(
        extent, rows_here, length, owners
    )
    edge = max(1, polys // SHARE)
    head = max(1, edge // 2)
    counts = (head, polys - head - edge, edge)
    starts = (0, head, polys - edge)

    def opened(i):
        return first_section(coefficients, first_tables, starts[i], counts[i], owners)

    def passed(sent):
        arrived = [sent[0]]
        for step in range(1, owners):
            order = [(i, (i + step) % owners) for i in range(owners)]
            arrived.append(lax.ppermute(sent[step], "coef", order))
        return arrived

    received = [passed(opened(0))]
    combined_here = column_sums(batch_weights, coefficients)
    received.append(passed(opened(1)))
    offsets = jnp.sum(batch_weights[None] * claimed, axis=2)
    offsets_here = lax.psum_scatter(
        offsets, ("poly", "limb"), scatter_dimension=1, tiled=True
    )
    quotient = quotient_section(
        combined_here, offsets_here, point_index, point_cycle, owners
    )
    received.append(passed(opened(2)))
    evaluations = second_section(received[0], second_tables, starts[0], polys, None)
    for i in (1, 2):
        evaluations = second_section(
            received[i], second_tables, starts[i], polys, evaluations
        )
    return (evaluations, quotient)


def solution(mesh):
    placed = (
        P(("parts", "poly", "limb"), None, "coef"),
        P("parts", ("poly", "limb")),
        P(None, "parts", ("poly", "limb")),
        P(("parts", "poly", "limb")),
        P(("parts", "poly", "limb")),
    )
    return jax.shard_map(
        functools.partial(shards, mesh.shape["coef"]),
        mesh=mesh,
        in_specs=placed,
        out_specs=(
            P(None, "coef", ("parts", "poly", "limb"), None, None),
            P(None, ("parts", "poly", "limb"), None, "coef"),
        ),
        check_vma=False,
    )
```
